32 devices in a mesh: grp: 2 (over x), tp: 16 (over z, y, core).
Axes of the slice: x: 2, y: 2, z: 4, core: 2. Of those that a mesh axis runs over, the one named last changes fastest.
Arguments:
- attn_in: bfloat16 [2, 4096, 8192], P(None, 'tp', 'grp'), parts along dimension 2, may hold values from -6 to 6
- attn_grad: bfloat16 [2, 4096, 8192], P(None, 'tp', 'grp'), parts along dimension 2, may hold values from -6 to 6
- ffn_in: bfloat16 [2, 14336, 8192], P(None, 'tp', 'grp'), parts along dimension 2, may hold values from -6 to 6
- ffn_grad: bfloat16 [2, 4096, 8192], P(None, 'tp', 'grp'), parts along dimension 2, may hold values from -6 to 6
- proj_attn_in: bfloat16 [2, 4096, 64], P(None, 'tp'), may hold values from -0.09375 to 0.09375
- proj_attn_out: bfloat16 [2, 4096, 64], P(None, 'tp'), may hold values from -0.09375 to 0.09375
- proj_ffn_in: bfloat16 [2, 14336, 64], P(None, 'tp'), may hold values from -0.046875 to 0.046875
- proj_ffn_out: bfloat16 [2, 4096, 64], P(None, 'tp'), may hold values from -0.09375 to 0.09375
- test_grads: bfloat16 [1024, 16384], P(None, 'tp'), may hold values from -0.0009765625 to 0.0009765625
Outputs:
- scores: float32 [4, 1024], P('grp'), parts along dimension 0
The draws below stay inside these ranges and needn't reach their ends.
There are 2 independent parts, one for each index of `grp`. The reference program is written for one: setup_inputs(seed, part) draws one part's arguments, and reference() takes and returns one part's arrays. A program takes and returns all parts, laid end to end along the dimension named above; an argument that names none is the same for every part. Nothing has to cross between parts.
All inputs are finite; a program needn't handle non-finite values.
Results may differ from the reference program's by a relative error of at most 0.0003.
Values may be sent and summed in bfloat16 or wider, within the bound.
No kernel may reach another device: no remote copies, remote signals or barrier semaphores. Data moves between devices by JAX's collectives and lax.ppermute only.
A program may use at most 192 MiB of HBM per device.

```python
import jax
import jax.numpy as jnp
from jax import lax

D = 4096
FF = 14336
K = 64
NTEST = 1024
LAYERS = 2
LEN = 2048
SEQS = 2
TOKENS = 4096
ENTRIES = 16384


def block_levels(own_key, dims, cuts, least, top_value):
    factor_of, own = 1.0, jax.random.fold_in(own_key, 6)
    for position, shards_of in cuts:
        steps = jnp.exp(jax.random.uniform(jax.random.fold_in(own, position), (shards_of,), jnp.float32, least / len(cuts), top_value / len(cuts)))
        factor_of = factor_of * jnp.repeat(steps, dims[position] // shards_of).reshape([-1 if axis == position else 1 for axis in range(len(dims))])
    return factor_of


def bell_draw(own_key, dims, scale, most, cuts=(), held_as=jnp.bfloat16):
    loudness = block_levels(own_key, dims, cuts, -0.22, 0.18) if cuts else 1.0
    result = jax.random.normal(own_key, dims, jnp.float32) * scale * loudness
    return jnp.minimum(jnp.maximum(result, -most), most).astype(held_as)


def setup_inputs(seed: int = 0, part: int = 0) -> dict:
    arg_keys = jax.random.split(jax.random.key(seed), 10)
    part_keys = jax.random.split(jax.random.fold_in(arg_keys[9], part), 10)
    return {
        "attn_in": bell_draw(part_keys[0], (LAYERS, D, TOKENS), 1.0, 6.0, ((1, 16),)),
        "attn_grad": bell_draw(part_keys[1], (LAYERS, D, TOKENS), 1.0, 6.0, ((1, 16),)),
        "ffn_in": bell_draw(part_keys[2], (LAYERS, FF, TOKENS), 1.0, 6.0, ((1, 16),)),
        "ffn_grad": bell_draw(part_keys[3], (LAYERS, D, TOKENS), 1.0, 6.0, ((1, 16),)),
        "proj_attn_in": bell_draw(arg_keys[4], (LAYERS, D, K), D ** -0.5, 0.09375, ((1, 16),)),
        "proj_attn_out": bell_draw(arg_keys[5], (LAYERS, D, K), D ** -0.5, 0.09375, ((1, 16),)),
        "proj_ffn_in": bell_draw(arg_keys[6], (LAYERS, FF, K), FF ** -0.5, 0.046875, ((1, 16),)),
        "proj_ffn_out": bell_draw(arg_keys[7], (LAYERS, D, K), D ** -0.5, 0.09375, ((1, 16),)),
        "test_grads": bell_draw(arg_keys[8], (NTEST, ENTRIES), (LAYERS * 2 * K * K * LEN) ** -0.5, 0.0009765625, ((1, 16),)),
    }


def project(acts, proj):
    return lax.dot_general(acts, proj, (((0,), (0,)), ((), ())), preferred_element_type=jnp.float32)


def per_sequence(grad_rows, input_rows):
    g = grad_rows.reshape(SEQS, LEN, K)
    x = input_rows.reshape(SEQS, LEN, K)
    outer = jnp.einsum("sta,stb->sab", g, x, precision=lax.Precision.HIGHEST)
    return outer.reshape(SEQS, K * K)


def reference(attn_in, attn_grad, ffn_in, ffn_grad, proj_attn_in, proj_attn_out, proj_ffn_in, proj_ffn_out, test_grads):
    pieces = []
    for layer in range(LAYERS):
        xa = project(attn_in[layer], proj_attn_in[layer])
        ga = project(attn_grad[layer], proj_attn_out[layer])
        xf = project(ffn_in[layer], proj_ffn_in[layer])
        gf = project(ffn_grad[layer], proj_ffn_out[layer])
        pieces.append(per_sequence(ga, xa))
        pieces.append(per_sequence(gf, xf))
    flat = jnp.concatenate(pieces, axis=1)
    tests = test_grads.astype(jnp.float32)
    return lax.dot_general(flat, tests, (((1,), (1,)), ((), ())), precision=lax.Precision.HIGHEST, preferred_element_type=jnp.float32)
```

```python
import functools

import jax
import jax.numpy as jnp
from jax import lax
from jax.experimental import pallas as pl
from jax.experimental.pallas import tpu as pltpu
from jax.sharding import PartitionSpec as P

LEN = 2048
SEQS = 2
K = 64
F32 = jnp.float32
BF16 = jnp.bfloat16
SPAN = 250.0
HIGH = lax.Precision.HIGHEST


def encode(values, codes_ref, row, scales_ref, index):
    top = jnp.max(jnp.abs(values), axis=0, keepdims=True)
    scale = (top * 1.015625).astype(BF16).astype(F32)
    scales_ref[index : index + 1, :] = scale
    factor = jnp.where(scale > 2e-36, SPAN / jnp.maximum(scale, 2e-36), 0.0)
    power = jnp.exp2(jnp.abs(values) * factor - 0.5 * SPAN)
    codes_ref[row : row + K, :] = jnp.where(values < 0, -power, power).astype(BF16)


def decode(codes_ref, row, scales, index):
    codes = codes_ref[row : row + K, :].astype(F32)
    scale = scales[index : index + 1, :] * (1.0 / SPAN)
    size = (jnp.log2(jnp.abs(codes)) + 0.5 * SPAN) * scale
    return jnp.where(codes < 0, -size, size)


def encode_rows(pieces, codes_ref, scales_ref):
    scales_ref[...] = jnp.zeros_like(scales_ref)
    for index, piece in enumerate(pieces):
        encode(piece, codes_ref, index * K, scales_ref, index)
    base = len(pieces) * K
    codes_ref[base : base + 16, :] = scales_ref[...].astype(BF16)


def read_scales(codes_ref, groups):
    return codes_ref[groups * K : groups * K + 16, :].astype(F32)


def project(l, m, which, acts, projs):
    a = acts[m * 2 + which]
    w = projs[m * 2 + which]
    return jnp.dot(w[l], a[l], preferred_element_type=F32)


def send_kernel(where_ref, a0, a1, a2, a3, w0, w1, w2, w3, out_ref):
    acts, projs = (a0, a1, a2, a3), (w0, w1, w2, w3)
    for l in range(2):
        for m in range(2):
            for which in range(2):
                row = ((l * 2 + m) * 2 + which) * K
                out_ref[row : row + K, :] = project(l, m, which, acts, projs)


def keep_y_kernel(where_ref, a0, a1, a2, a3, w0, w1, w2, w3, got_ref, codes_ref, kept_ref, scales_ref):
    acts, projs = (a0, a1, a2, a3), (w0, w1, w2, w3)
    step = pl.program_id(0)

    def pieces():
        for l in range(2):
            for m in range(2):
                for which in range(2):
                    row = ((l * 2 + m) * 2 + which) * K
                    yield project(l, m, which, acts, projs) + got_ref[row : row + K, :]

    @pl.when(step == 0)
    def _():
        encode_rows(list(pieces()), codes_ref, scales_ref)

    @pl.when(step == 1)
    def _():
        for index, piece in enumerate(pieces()):
            kept_ref[index // 4, (index // 2) % 2, (index % 2) * K : (index % 2) * K + K, :] = piece


def keep_z_kernel(where_ref, a0, a1, a2, a3, w0, w1, w2, w3, got_ref, codes_ref, kept_ref, total_ref, scales_ref):
    acts, projs = (a0, a1, a2, a3), (w0, w1, w2, w3)
    for l in range(2):
        for m in range(2):
            for which in range(2):
                row = ((l * 2 + m) * 2 + which) * K
                total_ref[l, m, which * K : which * K + K, :] = (
                    project(l, m, which, acts, projs) + got_ref[row : row + K, :]
                )
    mine = where_ref[2]
    other = 1 - mine
    encode_rows([total_ref[l, other, w * K : w * K + K, :] for l in range(2) for w in range(2)], codes_ref, scales_ref)
    for l in range(2):
        kept_ref[l] = total_ref[l, mine]


def half_m_kernel(where_ref, codes_in, kept_ref, codes_ref, out_ref, scales_ref, total_ref):
    mine = where_ref[2]
    other = 1 - mine
    scales = read_scales(codes_in, 8)
    for l in range(2):
        for m in range(2):
            for w in range(2):
                index = (l * 2 + m) * 2 + w
                rows = slice(w * K, w * K + K)
                total_ref[l, m, rows, :] = kept_ref[l, m, rows, :] + decode(codes_in, index * K, scales, index)
    encode_rows([total_ref[l, other, w * K : w * K + K, :] for l in range(2) for w in range(2)], codes_ref, scales_ref)
    for l in range(2):
        out_ref[l] = total_ref[l, mine]


def half_l_kernel(where_ref, codes_in, kept_ref, codes_ref, out_ref, scales_ref, total_ref):
    mine = where_ref[3]
    other = 1 - mine
    scales = read_scales(codes_in, 4)
    for l in range(2):
        for w in range(2):
            index = l * 2 + w
            rows = slice(w * K, w * K + K)
            total_ref[l, rows, :] = kept_ref[l, rows, :] + decode(codes_in, index * K, scales, index)
    encode_rows([total_ref[other, w * K : w * K + K, :] for w in range(2)], codes_ref, scales_ref)
    out_ref[...] = total_ref[mine]


def half_s_kernel(where_ref, codes_in, kept_ref, codes_ref, out_ref, scales_ref):
    step = pl.program_id(0)
    scales = read_scales(codes_in, 2)
    total = [kept_ref[w * K : w * K + K, :] + decode(codes_in, w * K, scales, w) for w in range(2)]

    @pl.when(step == 0)
    def _():
        encode_rows(total, codes_ref, scales_ref)

    @pl.when(step == 1)
    def _():
        for w in range(2):
            out_ref[w * K : w * K + K, :] = total[w]


def outer_kernel(codes_a, kept_a, codes_b, kept_b, out_ref):
    total = None
    for codes, kept in ((codes_a, kept_a), (codes_b, kept_b)):
        scales = read_scales(codes, 2)
        g, x = [kept[w * K : w * K + K, :] + decode(codes, w * K, scales, w) for w in range(2)]
        part = lax.dot_general(g, x, (((1,), (1,)), ((), ())), precision=HIGH, preferred_element_type=F32)
        total = part if total is None else total + part
    out_ref[...] = total


def cube(
    attn_in, attn_grad, ffn_in, ffn_grad, proj_attn_in, proj_attn_out, proj_ffn_in, proj_ffn_out, test_grads
):
    acts = (attn_grad, attn_in, ffn_grad, ffn_in)
    projs = tuple(w.transpose(0, 2, 1) for w in (proj_attn_out, proj_attn_in, proj_ffn_out, proj_ffn_in))
    total_tokens = attn_in.shape[2]
    block = total_tokens // 8
    me = lax.axis_index("tp")
    core, y, z = me % 2, (me // 2) % 2, me // 4
    where = jnp.stack([core, y, z % 2, z // 2]).astype(jnp.int32)

    def swap(value, bit):
        return lax.ppermute(value, "tp", [(i, i ^ bit) for i in range(16)])

    act_bytes = sum(a.shape[0] * a.shape[1] for a in acts) * 2 * block * 2
    flops = sum(a.shape[0] * a.shape[1] for a in acts) * 2 * block * 2 * K

    def run_acts(kernel, chunk, own, order, extra, outs, out_specs, scratch, name):
        def index(step, where_ref):
            c = where_ref[0] if own else 1 - where_ref[0]
            s = jnp.where(step == 0, 1 - where_ref[1], where_ref[1]) if order else step
            return (0, 0, s * 4 + c * 2 + chunk)

        def got_index(step, where_ref):
            s = jnp.where(step == 0, 1 - where_ref[1], where_ref[1]) if order else step
            return (0, s)

        in_specs = [pl.BlockSpec((a.shape[0], a.shape[1], block), index) for a in acts]
        in_specs += [pl.BlockSpec(w.shape, lambda i, r: (0, 0, 0)) for w in projs]
        if extra:
            in_specs.append(pl.BlockSpec((8 * K, block), got_index))
        return pl.pallas_call(
            kernel,
            out_shape=outs,
            grid_spec=pltpu.PrefetchScalarGridSpec(
                num_scalar_prefetch=1, grid=(2,), in_specs=in_specs, out_specs=out_specs, scratch_shapes=scratch
            ),
            cost_estimate=pl.CostEstimate(flops=flops, bytes_accessed=act_bytes, transcendentals=0),
            name=name,
        )(where, *acts, *projs, *extra)

    def sds(shape, dtype=F32):
        return jax.ShapeDtypeStruct(shape, dtype)

    def send(chunk):
        return run_acts(
            send_kernel, chunk, False, False, (), sds((8 * K, 2 * block)),
            pl.BlockSpec((8 * K, block), lambda i, r: (0, i)), [], f"send{chunk}",
        )

    scales_scratch = pltpu.VMEM((16, block), F32)

    def small(kernel, ins, outs, name, grid=None, in_specs=None, out_specs=None, scratch=(scales_scratch,), wide=block):
        vmem = pl.BlockSpec(memory_space=pltpu.VMEM)
        if grid is None:
            in_specs = [pl.BlockSpec(memory_space=pltpu.SMEM)] + [vmem] * len(ins)
            return pl.pallas_call(
                kernel, out_shape=outs, in_specs=in_specs, out_specs=[vmem] * len(outs),
                scratch_shapes=[pltpu.VMEM((16, wide), F32), pltpu.VMEM(ins[1].shape, F32)], name=name,
                cost_estimate=pl.CostEstimate(flops=0, bytes_accessed=4 << 20, transcendentals=0),
            )(where, *ins)
        return pl.pallas_call(
            kernel, out_shape=outs,
            grid_spec=pltpu.PrefetchScalarGridSpec(
                num_scalar_prefetch=1, grid=grid, in_specs=in_specs, out_specs=out_specs, scratch_shapes=list(scratch)
            ),
            cost_estimate=pl.CostEstimate(flops=0, bytes_accessed=2 << 20, transcendentals=0),
            name=name,
        )(where, *ins)

    got_a = swap(send(0), 1)
    got_b = swap(send(1), 1)

    codes_a, kept_a = run_acts(
        keep_y_kernel, 0, True, True, (got_a,),
        (sds((8 * K + 16, block), BF16), sds((2, 2, 2 * K, block))),
        [pl.BlockSpec((8 * K + 16, block), lambda i, r: (0, 0)), pl.BlockSpec((2, 2, 2 * K, block), lambda i, r: (0, 0, 0, 0))],
        [scales_scratch], "keep_a",
    )
    in_a = swap(codes_a, 2)
    codes_b, kept_b = run_acts(
        keep_z_kernel, 1, True, False, (got_b,),
        (sds((4 * K + 16, 2 * block), BF16), sds((2, 2 * K, 2 * block))),
        [pl.BlockSpec((4 * K + 16, block), lambda i, r: (0, i)), pl.BlockSpec((2, 2 * K, block), lambda i, r: (0, 0, i))],
        [pltpu.VMEM((2, 2, 2 * K, block), F32), scales_scratch], "keep_b",
    )
    in_b = swap(codes_b, 4)

    codes_a, kept_a = small(
        half_m_kernel, (in_a, kept_a), (sds((4 * K + 16, block), BF16), sds((2, 2 * K, block))), "half_m_a"
    )
    in_a = swap(codes_a, 4)
    codes_b, kept_b = small(
        half_l_kernel, (in_b, kept_b), (sds((2 * K + 16, 2 * block), BF16), sds((2 * K, 2 * block))), "half_l_b", wide=2 * block
    )
    in_b = swap(codes_b, 8)

    codes_a, kept_a = small(
        half_l_kernel, (in_a, kept_a), (sds((2 * K + 16, block), BF16), sds((2 * K, block))), "half_l_a"
    )
    in_a = swap(codes_a, 8)

    def by_s(step, r):
        return (0, jnp.where(step == 0, 1 - r[1], r[1]))

    codes_b, kept_b = small(
        half_s_kernel, (in_b, kept_b), (sds((2 * K + 16, block), BF16), sds((2 * K, block))), "half_s_b", grid=(2,),
        in_specs=[pl.BlockSpec((2 * K + 16, block), by_s), pl.BlockSpec((2 * K, block), by_s)],
        out_specs=[pl.BlockSpec((2 * K + 16, block), lambda i, r: (0, 0)), pl.BlockSpec((2 * K, block), lambda i, r: (0, 0))],
    )
    in_b = swap(codes_b, 2)

    outer = pl.pallas_call(
        outer_kernel, out_shape=sds((K, K)), name="outer",
        in_specs=[pl.BlockSpec(memory_space=pltpu.VMEM)] * 4, out_specs=pl.BlockSpec(memory_space=pltpu.VMEM),
    )(in_a, kept_a, in_b, kept_b)

    rows = outer.reshape(2, 2, K // 4, K)
    mine = lax.dynamic_index_in_dim(rows, core, 1, keepdims=False)
    other = lax.dynamic_index_in_dim(rows, 1 - core, 1, keepdims=False)
    mine = mine + swap(other, 1)
    here = lax.dynamic_index_in_dim(mine, y, 0, keepdims=False)
    there = swap(lax.dynamic_index_in_dim(mine, 1 - y, 0, keepdims=False), 2)
    first = jnp.where(y == 0, here, there)
    second = jnp.where(y == 0, there, here)
    flat = jnp.stack([first, second]).reshape(2, K // 4 * K)
    scores = lax.dot_general(
        flat, test_grads.astype(F32), (((1,), (1,)), ((), ())), precision=HIGH, preferred_element_type=F32
    )
    for bit in (1, 2, 4, 8):
        scores = scores + swap(scores, bit)
    return scores


def shards(
    attn_in, attn_grad, ffn_in, ffn_grad, proj_attn_in, proj_attn_out, proj_ffn_in, proj_ffn_out, test_grads
):
    layers, _, total = attn_in.shape
    devices = lax.axis_size("tp")
    modules = ((attn_grad, proj_attn_out, attn_in, proj_attn_in), (ffn_grad, proj_ffn_out, ffn_in, proj_ffn_in))
    columns = []
    for layer in range(layers):
        for grad, out, source, into in modules:
            for act, weight in ((grad, out), (source, into)):
                columns.append(
                    lax.dot_general(
                        weight[layer], act[layer], (((0,), (0,)), ((), ())), preferred_element_type=F32
                    )
                )
    rows = total // devices
    projected = lax.psum_scatter(jnp.concatenate(columns), "tp", scatter_dimension=1, tiled=True)
    token = lax.axis_index("tp") * rows + jnp.arange(rows, dtype=jnp.int32)
    member = (token // LEN)[None, :] == jnp.arange(SEQS, dtype=jnp.int32)[:, None]
    pairs = projected.reshape(2 * layers, 2, K, rows)
    grads = jnp.where(member[:, None, None, :], pairs[None, :, 0], 0.0)
    outer = jnp.einsum("snat,nbt->snab", grads, pairs[:, 1], precision=HIGH)
    flat = outer.reshape(SEQS, devices, -1).transpose(1, 0, 2)
    flat = flat.reshape(devices, -1)
    owned = lax.psum_scatter(flat, "tp", scatter_dimension=0, tiled=True).reshape(SEQS, -1)
    scores = lax.dot_general(
        owned, test_grads.astype(F32), (((1,), (1,)), ((), ())), precision=HIGH, preferred_element_type=F32
    )
    return lax.psum(scores, "tp")


def solution(mesh):
    placed = (P(None, "tp", "grp"),) * 4 + (P(None, "tp", None),) * 4 + (P(None, "tp"),)
    body = cube if mesh.shape["tp"] == 16 else shards
    return jax.shard_map(body, mesh=mesh, in_specs=placed, out_specs=P("grp", None), check_vma=False)
```

```python
import functools

import jax
import jax.numpy as jnp
from jax import lax
from jax.experimental import pallas as pl
from jax.experimental.pallas import tpu as pltpu
from jax.sharding import PartitionSpec as P

LEN = 2048
SEQS = 2
K = 64
F32 = jnp.float32
BF16 = jnp.bfloat16
SPAN = 250.0
HIGH = lax.Precision.HIGHEST


def encode(values, codes_ref, row, scales_ref, index):
    top = jnp.max(jnp.abs(values), axis=0, keepdims=True)
    scale = (top * 1.015625).astype(BF16).astype(F32)
    scales_ref[index : index + 1, :] = scale
    factor = jnp.where(scale > 2e-36, SPAN / jnp.maximum(scale, 2e-36), 0.0)
    power = jnp.exp2(jnp.abs(values) * factor - 0.5 * SPAN)
    codes_ref[row : row + K, :] = jnp.where(values < 0, -power, power).astype(BF16)


def decode(codes_ref, row, scales, index):
    codes = codes_ref[row : row + K, :].astype(F32)
    scale = scales[index : index + 1, :] * (1.0 / SPAN)
    size = (jnp.log2(jnp.abs(codes)) + 0.5 * SPAN) * scale
    return jnp.where(codes < 0, -size, size)


def encode_groups(groups, codes_ref, scales_ref):
    scales_ref[...] = jnp.zeros_like(scales_ref)
    for index, values in enumerate(groups):
        encode(values, codes_ref, index * K, scales_ref, index)
    codes_ref[len(groups) * K :, :] = scales_ref[...].astype(BF16)


def split(dim, total_ref, codes_ref, kept_ref, scales_ref, where_ref):
    layers, modules, _, tokens = total_ref.shape
    mine = where_ref[" sml".index(dim)]
    other = 1 - mine
    if dim == "s":
        width = tokens // 2
        leave = pl.ds(pl.multiple_of(other * width, 128), width)
        stay = pl.ds(pl.multiple_of(mine * width, 128), width)
        groups = [(l, m, w, leave) for l in range(layers) for m in range(modules) for w in range(2)]
    elif dim == "m":
        groups = [(l, other, w, slice(None)) for l in range(layers) for w in range(2)]
    else:
        groups = [(other, m, w, slice(None)) for m in range(modules) for w in range(2)]
    encode_groups(
        [total_ref[l, m, w * K : w * K + K, lanes] for l, m, w, lanes in groups], codes_ref, scales_ref
    )
    if dim == "s":
        kept_ref[...] = total_ref[:, :, :, stay]
    elif dim == "m":
        for l in range(layers):
            kept_ref[l, 0] = total_ref[l, mine]
    else:
        kept_ref[0] = total_ref[mine]


def add_codes(codes_ref, kept_ref, total_ref):
    layers, modules, _, _ = kept_ref.shape
    rows = layers * modules * 2 * K
    scales = codes_ref[rows:, :].astype(F32)
    for l in range(layers):
        for m in range(modules):
            for w in range(2):
                index = (l * modules + m) * 2 + w
                part = slice(w * K, w * K + K)
                total_ref[l, m, part, :] = kept_ref[l, m, part, :] + decode(codes_ref, index * K, scales, index)


def split_kernel(dim, where_ref, codes_in, kept_in, codes_ref, kept_ref, scales_ref, total_ref):
    add_codes(codes_in, kept_in, total_ref)
    split(dim, total_ref, codes_ref, kept_ref, scales_ref, where_ref)


def outer_kernel(chunks, where_ref, *refs):
    ins, (leave_ref, stay_ref), totals = refs[: 2 * chunks], refs[2 * chunks : 2 * chunks + 2], refs[2 * chunks + 2 :]
    out_ref, totals = totals[0], totals[1:]
    total = None
    for chunk in range(chunks):
        sums = totals[chunk]
        add_codes(ins[2 * chunk], ins[2 * chunk + 1], sums)
        part = lax.dot_general(
            sums[0, 0, :K, :], sums[0, 0, K:, :], (((1,), (1,)), ((), ())), precision=HIGH, preferred_element_type=F32
        )
        total = part if total is None else total + part
    out_ref[...] = total
    core = where_ref[0]
    quarter = K // 4
    for y in range(2):
        leave_ref[y] = out_ref[pl.ds(pl.multiple_of((2 * y + 1 - core) * quarter, 8), quarter), :]
        stay_ref[y] = out_ref[pl.ds(pl.multiple_of((2 * y + core) * quarter, 8), quarter), :]


def scores_kernel(flat_ref, tests_ref, out_ref):
    rest = flat_ref[...]
    parts = []
    for _ in range(3):
        part = rest.astype(BF16)
        parts.append(part)
        rest = rest - part.astype(F32)
    total = None
    for part in reversed(parts):
        term = lax.dot_general(part, tests_ref[...], (((1,), (1,)), ((), ())), preferred_element_type=F32)
        total = term if total is None else total + term
    out_ref[...] = total


def project_kernel(own, where_ref, *refs):
    chunks = len(refs) - 17
    acts, projs, outs = refs[:4], refs[4:8], refs[8 : 8 + chunks]
    act_bufs, proj_bufs, sems = refs[8 + chunks : 12 + chunks], refs[12 + chunks : 16 + chunks], refs[16 + chunks]
    core = where_ref[0] if own else 1 - where_ref[0]
    layers, _, total = acts[0].shape
    quarter = total // 4
    pieces = [(s, l, i) for s in range(2) for l in range(layers) for i in range(4)]
    loads = [pltpu.make_async_copy(projs[i], proj_bufs[i], sems.at[len(pieces) + i]) for i in range(4)]
    copies = []
    for index, (s, l, i) in enumerate(pieces):
        lanes = pl.ds(pl.multiple_of(s * (total // 2) + core * quarter, 128), quarter)
        copies.append(pltpu.make_async_copy(acts[i].at[l, :, lanes], act_bufs[i].at[s, l], sems.at[index]))
    for copy in loads + copies:
        copy.start()
    for copy in loads:
        copy.wait()
    for index, (s, l, i) in enumerate(pieces):
        copies[index].wait()
        at = 0
        for out_ref in outs:
            width = out_ref.shape[-1] // 2
            out_ref[l, i // 2, i % 2 * K : i % 2 * K + K, s * width : (s + 1) * width] = jnp.dot(
                proj_bufs[i][l], act_bufs[i][s, l, :, at : at + width], preferred_element_type=F32
            )
            at += width


def join_kernel(dim, where_ref, own_ref, got_ref, codes_ref, kept_ref, scales_ref, total_ref):
    total_ref[...] = own_ref[...] + got_ref[...]
    split(dim, total_ref, codes_ref, kept_ref, scales_ref, where_ref)


CHUNKS = ((512, 'sml'), (512, 'msl'))
BITS = {"s": 2, "m": 4, "l": 8}


def cube(
    attn_in, attn_grad, ffn_in, ffn_grad, proj_attn_in, proj_attn_out, proj_ffn_in, proj_ffn_out, test_grads
):
    acts = (attn_grad, attn_in, ffn_grad, ffn_in)
    projs = tuple(w.transpose(0, 2, 1) for w in (proj_attn_out, proj_attn_in, proj_ffn_out, proj_ffn_in))
    acts = tuple(pltpu.with_memory_space_constraint(a, pltpu.HBM) for a in acts)
    projs = tuple(pltpu.with_memory_space_constraint(a, pltpu.HBM) for a in projs)
    quarter = attn_in.shape[2] // 4
    me = lax.axis_index("tp")
    core, y, z = me % 2, (me // 2) % 2, me // 4
    where = jnp.stack([core, y, z % 2, z // 2]).astype(jnp.int32)
    smem = pl.BlockSpec(memory_space=pltpu.SMEM)
    vmem = pl.BlockSpec(memory_space=pltpu.VMEM)
    hbm = pl.BlockSpec(memory_space=pltpu.HBM)

    def swap(value, bit):
        return lax.ppermute(value, "tp", [(i, i ^ bit) for i in range(16)])

    def sds(shape, dtype=F32):
        return jax.ShapeDtypeStruct(shape, dtype)

    def call(kernel, ins, in_specs, outs, scratch, name, cost, limit):
        nonlocal where

        def chained(where_ref, *refs):
            passed = refs[len(ins)]
            for i in range(4):
                passed[i] = where_ref[i]
            kernel(where_ref, *refs[: len(ins)], *refs[len(ins) + 1 :])

        where, *results = pl.pallas_call(
            chained, out_shape=(sds((4,), jnp.int32), *outs), in_specs=[smem] + in_specs,
            out_specs=[smem] + [vmem] * len(outs), scratch_shapes=scratch,
            name=name, cost_estimate=pl.CostEstimate(flops=0, bytes_accessed=cost, transcendentals=0),
            compiler_params=pltpu.CompilerParams(vmem_limit_bytes=limit << 20),
        )(where, *ins)
        return results

    def outputs(dim, shape):
        layers, modules, _, tokens = shape
        kept = {
            "s": (layers, modules, 2 * K, tokens // 2), "m": (layers, 1, 2 * K, tokens), "l": (1, modules, 2 * K, tokens)
        }[dim]
        groups = kept[0] * kept[1] * 2
        scales = max(8, groups)
        return (sds((groups * K + scales, kept[3]), BF16), sds(kept)), pltpu.VMEM((scales, kept[3]), F32)

    def project(name, own):
        scratch = [pltpu.VMEM((2, a.shape[0], a.shape[1], quarter), BF16) for a in acts]
        scratch += [pltpu.VMEM(w.shape, BF16) for w in projs] + [pltpu.SemaphoreType.DMA((8 * acts[0].shape[0] + 4,))]
        outs = tuple(sds((2, 2, 2 * K, 2 * width)) for width, _ in CHUNKS)
        return call(
            functools.partial(project_kernel, own), (*acts, *projs), [hbm] * 8, outs, scratch, name, 16 << 20, 24
        )

    def join(index, own, got, dim):
        outs, scales = outputs(dim, own.shape)
        return call(
            functools.partial(join_kernel, dim), (own, got), [vmem] * 2, outs, [scales, pltpu.VMEM(own.shape, F32)],
            f"join{index}{dim}", 4 << 20, 12,
        )

    def exchange(index, codes, kept, dim):
        outs, scales = outputs(dim, kept.shape)
        return call(
            functools.partial(split_kernel, dim), (codes, kept), [vmem] * 2, outs,
            [scales, pltpu.VMEM(kept.shape, F32)], f"split{index}{dim}", 4 << 20, 12,
        )

    sent = project("send", False)
    with jax.named_scope("cores"):
        got = [swap(value, 1) for value in sent]
    own = project("own", True)
    state = []
    for i, (_, order) in enumerate(CHUNKS):
        codes, kept = join(i, own[i], got[i], order[0])
        with jax.named_scope(f"x{i}{order[0]}"):
            state.append((swap(codes, BITS[order[0]]), kept))
    for stage in (1, 2):
        for i, (_, order) in enumerate(CHUNKS):
            codes, kept = exchange(i, *state[i], order[stage])
            with jax.named_scope(f"x{i}{order[stage]}"):
                state[i] = (swap(codes, BITS[order[stage]]), kept)


    leave, stay = call(
        functools.partial(outer_kernel, len(CHUNKS)), sum(((g, k) for g, k in state), ()), [vmem] * (2 * len(CHUNKS)),
        (sds((2, K // 4, K)), sds((2, K // 4, K))),
        [pltpu.VMEM((K, K), F32)] + [pltpu.VMEM(k.shape, F32) for _, k in state], "outer", 2 << 20, 12,
    )
    mine = stay + swap(leave, 1)
    here = lax.dynamic_index_in_dim(mine, y, 0, keepdims=False)
    there = swap(lax.dynamic_index_in_dim(mine, 1 - y, 0, keepdims=False), 2)
    first = jnp.where(y == 0, here, there)
    second = jnp.where(y == 0, there, here)
    flat = jnp.stack([first, second]).reshape(2, K // 4 * K)
    scores = pl.pallas_call(
        scores_kernel, out_shape=sds((2, test_grads.shape[0])), in_specs=[vmem] * 2, out_specs=vmem, name="scores",
        compiler_params=pltpu.CompilerParams(vmem_limit_bytes=12 << 20),
    )(flat, test_grads)
    for bit in (1, 2, 4, 8):
        scores = scores + swap(scores, bit)
    return scores


def shards(
    attn_in, attn_grad, ffn_in, ffn_grad, proj_attn_in, proj_attn_out, proj_ffn_in, proj_ffn_out, test_grads
):
    layers, _, total = attn_in.shape
    devices = lax.axis_size("tp")
    modules = ((attn_grad, proj_attn_out, attn_in, proj_attn_in), (ffn_grad, proj_ffn_out, ffn_in, proj_ffn_in))
    columns = []
    for layer in range(layers):
        for grad, out, source, into in modules:
            for act, weight in ((grad, out), (source, into)):
                columns.append(
                    lax.dot_general(
                        weight[layer], act[layer], (((0,), (0,)), ((), ())), preferred_element_type=F32
                    )
                )
    rows = total // devices
    projected = lax.psum_scatter(jnp.concatenate(columns), "tp", scatter_dimension=1, tiled=True)
    token = lax.axis_index("tp") * rows + jnp.arange(rows, dtype=jnp.int32)
    member = (token // LEN)[None, :] == jnp.arange(SEQS, dtype=jnp.int32)[:, None]
    pairs = projected.reshape(2 * layers, 2, K, rows)
    grads = jnp.where(member[:, None, None, :], pairs[None, :, 0], 0.0)
    outer = jnp.einsum("snat,nbt->snab", grads, pairs[:, 1], precision=HIGH)
    flat = outer.reshape(SEQS, devices, -1).transpose(1, 0, 2)
    flat = flat.reshape(devices, -1)
    owned = lax.psum_scatter(flat, "tp", scatter_dimension=0, tiled=True).reshape(SEQS, -1)
    scores = lax.dot_general(
        owned, test_grads.astype(F32), (((1,), (1,)), ((), ())), precision=HIGH, preferred_element_type=F32
    )
    return lax.psum(scores, "tp")


def solution(mesh):
    placed = (P(None, "tp", "grp"),) * 4 + (P(None, "tp", None),) * 4 + (P(None, "tp"),)
    body = cube if mesh.shape["tp"] == 16 else shards
    return jax.shard_map(body, mesh=mesh, in_specs=placed, out_specs=P("grp", None), check_vma=False)
```

```python
import functools

import jax
import jax.numpy as jnp
from jax import lax
from jax.experimental import pallas as pl
from jax.experimental.pallas import tpu as pltpu
from jax.sharding import PartitionSpec as P


LEN = 2048
SEQS = 2
K = 64
F32 = jnp.float32
BF16 = jnp.bfloat16
SPAN = 250.0
HIGH = lax.Precision.HIGHEST


def encode(values, codes_ref, row, scales_ref, index):
    top = jnp.max(jnp.abs(values), axis=0, keepdims=True)
    scale = (top * 1.015625).astype(BF16).astype(F32)
    scales_ref[index : index + 1, :] = scale
    factor = jnp.where(scale > 2e-36, SPAN / jnp.maximum(scale, 2e-36), 0.0)
    power = jnp.exp2(jnp.abs(values) * factor - 0.5 * SPAN)
    codes_ref[row : row + K, :] = jnp.where(values < 0, -power, power).astype(BF16)


def decode(codes_ref, row, scales, index):
    codes = codes_ref[row : row + K, :].astype(F32)
    scale = scales[index : index + 1, :] * (1.0 / SPAN)
    size = (jnp.log2(jnp.abs(codes)) + 0.5 * SPAN) * scale
    return jnp.where(codes < 0, -size, size)


def encode_groups(groups, codes_ref, scales_ref):
    scales_ref[...] = jnp.zeros_like(scales_ref)
    for index, values in enumerate(groups):
        encode(values, codes_ref, index * K, scales_ref, index)
    codes_ref[len(groups) * K :, :] = scales_ref[...].astype(BF16)


def split(dim, total_ref, codes_ref, kept_ref, scales_ref, where_ref):
    layers, modules, _, tokens = total_ref.shape
    mine = where_ref[" sml".index(dim)]
    other = 1 - mine
    if dim == "s":
        width = tokens // 2
        leave = pl.ds(pl.multiple_of(other * width, 128), width)
        stay = pl.ds(pl.multiple_of(mine * width, 128), width)
        groups = [(l, m, w, leave) for l in range(layers) for m in range(modules) for w in range(2)]
    elif dim == "m":
        groups = [(l, other, w, slice(None)) for l in range(layers) for w in range(2)]
    else:
        groups = [(other, m, w, slice(None)) for m in range(modules) for w in range(2)]
    encode_groups(
        [total_ref[l, m, w * K : w * K + K, lanes] for l, m, w, lanes in groups], codes_ref, scales_ref
    )
    if dim == "s":
        kept_ref[...] = total_ref[:, :, :, stay]
    elif dim == "m":
        for l in range(layers):
            kept_ref[l, 0] = total_ref[l, mine]
    else:
        kept_ref[0] = total_ref[mine]


def add_codes(codes_ref, kept_ref, total_ref):
    layers, modules, _, _ = kept_ref.shape
    rows = layers * modules * 2 * K
    scales = codes_ref[rows:, :].astype(F32)
    for l in range(layers):
        for m in range(modules):
            for w in range(2):
                index = (l * modules + m) * 2 + w
                part = slice(w * K, w * K + K)
                total_ref[l, m, part, :] = kept_ref[l, m, part, :] + decode(codes_ref, index * K, scales, index)


def split_kernel(dim, where_ref, codes_in, kept_in, codes_ref, kept_ref, scales_ref, total_ref):
    add_codes(codes_in, kept_in, total_ref)
    split(dim, total_ref, codes_ref, kept_ref, scales_ref, where_ref)


def products(ins, totals):
    total = None
    for chunk, sums in enumerate(totals):
        add_codes(ins[2 * chunk], ins[2 * chunk + 1], sums)
        part = lax.dot_general(
            sums[0, 0, :K, :], sums[0, 0, K:, :], (((1,), (1,)), ((), ())), precision=HIGH, preferred_element_type=F32
        )
        total = part if total is None else total + part
    return total


def early_kernel(where_ref, tests_in, *refs):
    chunks = (len(refs) - 3) // 3
    sum_ref, tests_ref, sem = refs[2 * chunks], refs[2 * chunks + 1], refs[-1]
    copy = pltpu.make_async_copy(tests_in, tests_ref, sem)
    copy.start()
    sum_ref[...] = products(refs[: 2 * chunks], refs[2 * chunks + 2 : -1])
    copy.wait()


def outer_kernel(where_ref, early_ref, *refs):
    chunks = (len(refs) - 3) // 3
    leave_ref, stay_ref, out_ref = refs[2 * chunks : 2 * chunks + 3]
    out_ref[...] = early_ref[...] + products(refs[: 2 * chunks], refs[2 * chunks + 3 :])
    core = where_ref[0]
    quarter = K // 4
    for y in range(2):
        leave_ref[y] = out_ref[pl.ds(pl.multiple_of((2 * y + 1 - core) * quarter, 8), quarter), :]
        stay_ref[y] = out_ref[pl.ds(pl.multiple_of((2 * y + core) * quarter, 8), quarter), :]


def scores_kernel(flat_ref, tests_ref, out_ref):
    rest = flat_ref[...]
    rows = rest.shape[0]
    parts = []
    for _ in range(3):
        part = rest.astype(BF16)
        parts.append(part)
        rest = rest - part.astype(F32)
    terms = lax.dot_general(
        jnp.concatenate(parts, axis=0), tests_ref[...], (((1,), (1,)), ((), ())), preferred_element_type=F32
    )
    out_ref[...] = terms[2 * rows :] + terms[rows : 2 * rows] + terms[:rows]


def project_kernel(own, first, ahead, after, where_ref, *refs):
    acts, projs, refs = refs[:4], refs[4:8], refs[8:]
    given, refs = refs[:ahead], refs[ahead:]
    proj_bufs, sems, act_bufs = refs[-5:-1], refs[-1], refs[-9:-5]
    outs, fetched = refs[: -9 - after], refs[len(refs) - 9 - after : -9]
    layers, _, total = acts[0].shape
    quarter = total // 4
    width = act_bufs[0].shape[-1]
    pieces = [(s, l, i) for s in range(2) for l in range(layers) for i in range(4)]

    def fetch(index, core, target, sem):
        s, l, i = pieces[index]
        lanes = pl.ds(pl.multiple_of(s * (total // 2) + core * quarter + first, 128), width)
        copy = pltpu.make_async_copy(acts[i].at[l, :, lanes], target, sem)
        copy.start()
        return copy

    core = where_ref[0] if own else 1 - where_ref[0]
    copies = {}
    loads = [pltpu.make_async_copy(projs[i], proj_bufs[i], sems.at[len(pieces) + i]) for i in range(4)]
    for copy in loads:
        copy.start()
    for index in range(ahead, len(pieces)):
        s, l, i = pieces[index]
        copies[index] = fetch(index, core, act_bufs[i].at[s, l], sems.at[index])
    later = [fetch(j, where_ref[0], fetched[j], sems.at[len(pieces) + 4 + j]) for j in range(after)]
    for copy in loads:
        copy.wait()
    for index, (s, l, i) in enumerate(pieces):
        if index in copies:
            copies[index].wait()
        act = act_bufs[i][s, l] if index in copies else given[index][...]
        value = jnp.dot(proj_bufs[i][l], act, preferred_element_type=F32)
        at = 0
        for out_ref in outs:
            span = out_ref.shape[-1] // 2
            out_ref[l, i // 2, i % 2 * K : i % 2 * K + K, s * span : (s + 1) * span] = value[:, at : at + span]
            at += span
    for copy in later:
        copy.wait()


def join_kernel(dim, where_ref, own_ref, got_ref, codes_ref, kept_ref, scales_ref, total_ref):
    total_ref[...] = own_ref[...] + got_ref[...]
    split(dim, total_ref, codes_ref, kept_ref, scales_ref, where_ref)


CHUNKS = ((384, 'sml'), (384, 'msl'), (256, 'sml'))
PLAN = (('send', 0, (0, 1, 2)), ('own', 0, (0, 1, 2)), ('k', 0, 0), ('x', 0, 0), ('k', 1, 0), ('x', 1, 0), ('k', 2, 0), ('x', 2, 0), ('k', 0, 1), ('x', 0, 1), ('k', 1, 1), ('x', 1, 1), ('k', 2, 1), ('x', 2, 1), ('k', 0, 2), ('x', 0, 2), ('k', 1, 2), ('x', 1, 2), ('k', 2, 2), ('x', 2, 2))
AFTER = 4
EARLY = 1
FINISH = tuple(i for kind, i, stage in PLAN if kind == "x" and stage == 2)
BITS = {"s": 2, "m": 4, "l": 8}


def cube_body(
    attn_in, attn_grad, ffn_in, ffn_grad, proj_attn_in, proj_attn_out, proj_ffn_in, proj_ffn_out, test_grads
):
    acts = (attn_grad, attn_in, ffn_grad, ffn_in)
    projs = tuple(w.transpose(0, 2, 1) for w in (proj_attn_out, proj_attn_in, proj_ffn_out, proj_ffn_in))
    acts = tuple(pltpu.with_memory_space_constraint(a, pltpu.HBM) for a in acts)
    projs = tuple(pltpu.with_memory_space_constraint(a, pltpu.HBM) for a in projs)
    me = lax.axis_index("tp")
    core, y, z = me % 2, (me // 2) % 2, me // 4
    where = jnp.stack([core, y, z % 2, z // 2]).astype(jnp.int32)
    smem = pl.BlockSpec(memory_space=pltpu.SMEM)
    vmem = pl.BlockSpec(memory_space=pltpu.VMEM)
    hbm = pl.BlockSpec(memory_space=pltpu.HBM)

    def swap(value, bit):
        return lax.ppermute(value, "tp", [(i, i ^ bit) for i in range(16)])

    def sds(shape, dtype=F32):
        return jax.ShapeDtypeStruct(shape, dtype)

    def call(kernel, ins, in_specs, outs, scratch, cost, limit):
        return pl.pallas_call(
            kernel, out_shape=outs, in_specs=[smem] + in_specs, out_specs=[vmem] * len(outs), scratch_shapes=scratch,
            cost_estimate=pl.CostEstimate(flops=0, bytes_accessed=cost, transcendentals=0),
            compiler_params=pltpu.CompilerParams(vmem_limit_bytes=limit << 20),
        )(where, *ins)

    def outputs(dim, shape):
        layers, modules, _, tokens = shape
        kept = {
            "s": (layers, modules, 2 * K, tokens // 2), "m": (layers, 1, 2 * K, tokens), "l": (1, modules, 2 * K, tokens)
        }[dim]
        groups = kept[0] * kept[1] * 2
        scales = max(8, groups)
        return (sds((groups * K + scales, kept[3]), BF16), sds(kept)), pltpu.VMEM((scales, kept[3]), F32)

    def project(own, chunks, given=(), after=0):
        widths = [CHUNKS[i][0] for i in chunks]
        first = sum(width for width, _ in CHUNKS[: chunks[0]])
        width = sum(widths)
        layers = acts[0].shape[0]
        scratch = [pltpu.VMEM((2, layers, a.shape[1], width), BF16) for a in acts]
        scratch += [pltpu.VMEM(w.shape, BF16) for w in projs] + [pltpu.SemaphoreType.DMA((8 * layers + 4 + after,))]
        outs = tuple(sds((2, 2, 2 * K, 2 * width)) for width in widths)
        outs += tuple(sds((acts[i % 4].shape[1], width), BF16) for i in range(after))
        results = call(
            functools.partial(project_kernel, own, first, len(given), after), (*acts, *projs, *given),
            [hbm] * 8 + [vmem] * len(given), outs, scratch, 16 << 20, 26,
        )
        return results[: len(widths)], results[len(widths) :]

    def join(own, got, dim):
        outs, scales = outputs(dim, own.shape)
        return call(
            functools.partial(join_kernel, dim), (own, got), [vmem] * 2, outs, [scales, pltpu.VMEM(own.shape, F32)],
            4 << 20, 12,
        )

    def exchange(codes, kept, dim):
        outs, scales = outputs(dim, kept.shape)
        return call(
            functools.partial(split_kernel, dim), (codes, kept), [vmem] * 2, outs,
            [scales, pltpu.VMEM(kept.shape, F32)], 4 << 20, 12,
        )

    got, own, state, ready = {}, {}, {}, ()
    for step in PLAN:
        kind, i, stage = step
        if kind == "send":
            sent, ready = project(False, stage, (), AFTER)
            for j, value in zip(stage, sent):
                got[j] = swap(value, 1)
        elif kind == "own":
            made, _ = project(True, stage, ready)
            own.update(zip(stage, made))
            ready = ()
        elif kind == "k" and stage == 0:
            state[i] = join(own[i], got[i], CHUNKS[i][1][0])
        elif kind == "k":
            state[i] = exchange(*state[i], CHUNKS[i][1][stage])
        else:
            dim = CHUNKS[i][1][stage]
            state[i] = (swap(state[i][0], BITS[dim]), state[i][1])
    state = [tuple(state[i]) for i in range(len(CHUNKS))]


    before, last = [state[i] for i in FINISH[:EARLY]], [state[i] for i in FINISH[EARLY:]]
    tests = pltpu.with_memory_space_constraint(test_grads, pltpu.HBM)
    early, tests = call(
        early_kernel, (tests, *sum(before, ())), [hbm] + [vmem] * (2 * len(before)),
        (sds((K, K)), sds(tests.shape, tests.dtype)),
        [pltpu.VMEM(k.shape, F32) for _, k in before] + [pltpu.SemaphoreType.DMA], 4 << 20, 12,
    )
    leave, stay = call(
        outer_kernel, (early, *sum(last, ())), [vmem] * (1 + 2 * len(last)), (sds((2, K // 4, K)), sds((2, K // 4, K))),
        [pltpu.VMEM((K, K), F32)] + [pltpu.VMEM(k.shape, F32) for _, k in last], 2 << 20, 12,
    )
    mine = stay + swap(leave, 1)
    here = lax.dynamic_index_in_dim(mine, y, 0, keepdims=False)
    there = swap(lax.dynamic_index_in_dim(mine, 1 - y, 0, keepdims=False), 2)
    first = jnp.where(y == 0, here, there)
    second = jnp.where(y == 0, there, here)
    flat = jnp.stack([first, second]).reshape(2, K // 4 * K)
    scores = pl.pallas_call(
        scores_kernel, out_shape=sds((2, test_grads.shape[0])), in_specs=[vmem] * 2, out_specs=vmem, name="scores",
        compiler_params=pltpu.CompilerParams(vmem_limit_bytes=12 << 20),
    )(flat, tests)
    for bit in (1, 2, 4, 8):
        scores = scores + swap(scores, bit)
    return scores


def cube(*args):
    return cube_body(*args)


def shards(
    attn_in, attn_grad, ffn_in, ffn_grad, proj_attn_in, proj_attn_out, proj_ffn_in, proj_ffn_out, test_grads
):
    layers, _, total = attn_in.shape
    devices = lax.axis_size("tp")
    modules = ((attn_grad, proj_attn_out, attn_in, proj_attn_in), (ffn_grad, proj_ffn_out, ffn_in, proj_ffn_in))
    columns = []
    for layer in range(layers):
        for grad, out, source, into in modules:
            for act, weight in ((grad, out), (source, into)):
                columns.append(
                    lax.dot_general(
                        weight[layer], act[layer], (((0,), (0,)), ((), ())), preferred_element_type=F32
                    )
                )
    rows = total // devices
    projected = lax.psum_scatter(jnp.concatenate(columns), "tp", scatter_dimension=1, tiled=True)
    token = lax.axis_index("tp") * rows + jnp.arange(rows, dtype=jnp.int32)
    member = (token // LEN)[None, :] == jnp.arange(SEQS, dtype=jnp.int32)[:, None]
    pairs = projected.reshape(2 * layers, 2, K, rows)
    grads = jnp.where(member[:, None, None, :], pairs[None, :, 0], 0.0)
    outer = jnp.einsum("snat,nbt->snab", grads, pairs[:, 1], precision=HIGH)
    flat = outer.reshape(SEQS, devices, -1).transpose(1, 0, 2)
    flat = flat.reshape(devices, -1)
    owned = lax.psum_scatter(flat, "tp", scatter_dimension=0, tiled=True).reshape(SEQS, -1)
    scores = lax.dot_general(
        owned, test_grads.astype(F32), (((1,), (1,)), ((), ())), precision=HIGH, preferred_element_type=F32
    )
    return lax.psum(scores, "tp")


def solution(mesh):
    placed = (P(None, "tp", "grp"),) * 4 + (P(None, "tp", None),) * 4 + (P(None, "tp"),)
    cubic = mesh.shape["tp"] == 16
    return jax.shard_map(
        cube if cubic else shards, mesh=mesh, in_specs=placed, out_specs=P("grp", None), check_vma=False
    )
```

```python
import functools

import jax
import jax.numpy as jnp
from jax import lax
from jax.experimental import pallas as pl
from jax.experimental.pallas import tpu as pltpu
from jax.sharding import PartitionSpec as P


LEN = 2048
SEQS = 2
K = 64
F32 = jnp.float32
BF16 = jnp.bfloat16
SPAN = 250.0
HIGH = lax.Precision.HIGHEST


def encode(values, codes_ref, row, scales_ref, index):
    top = jnp.max(jnp.abs(values), axis=0, keepdims=True)
    scale = (top * 1.015625).astype(BF16).astype(F32)
    scales_ref[index : index + 1, :] = scale
    factor = jnp.where(scale > 2e-36, SPAN / jnp.maximum(scale, 2e-36), 0.0)
    power = jnp.exp2(jnp.abs(values) * factor - 0.5 * SPAN)
    codes_ref[row : row + K, :] = jnp.where(values < 0, -power, power).astype(BF16)


def decode(codes_ref, row, scales, index):
    codes = codes_ref[row : row + K, :].astype(F32)
    scale = scales[index : index + 1, :] * (1.0 / SPAN)
    size = (jnp.log2(jnp.abs(codes)) + 0.5 * SPAN) * scale
    return jnp.where(codes < 0, -size, size)


def encode_groups(groups, codes_ref, scales_ref):
    scales_ref[...] = jnp.zeros_like(scales_ref)
    for index, values in enumerate(groups):
        encode(values, codes_ref, index * K, scales_ref, index)
    codes_ref[len(groups) * K :, :] = scales_ref[...].astype(BF16)


def split(dim, total_ref, codes_ref, kept_ref, scales_ref, where_ref):
    layers, modules, _, tokens = total_ref.shape
    mine = where_ref[" sml".index(dim)]
    other = 1 - mine
    if dim == "s":
        width = tokens // 2
        leave = pl.ds(pl.multiple_of(other * width, 128), width)
        stay = pl.ds(pl.multiple_of(mine * width, 128), width)
        groups = [(l, m, w, leave) for l in range(layers) for m in range(modules) for w in range(2)]
    elif dim == "m":
        groups = [(l, other, w, slice(None)) for l in range(layers) for w in range(2)]
    else:
        groups = [(other, m, w, slice(None)) for m in range(modules) for w in range(2)]
    encode_groups(
        [total_ref[l, m, w * K : w * K + K, lanes] for l, m, w, lanes in groups], codes_ref, scales_ref
    )
    if dim == "s":
        kept_ref[...] = total_ref[:, :, :, stay]
    elif dim == "m":
        for l in range(layers):
            kept_ref[l, 0] = total_ref[l, mine]
    else:
        kept_ref[0] = total_ref[mine]


def add_codes(codes_ref, kept_ref, total_ref):
    layers, modules, _, _ = kept_ref.shape
    rows = layers * modules * 2 * K
    scales = codes_ref[rows:, :].astype(F32)
    for l in range(layers):
        for m in range(modules):
            for w in range(2):
                index = (l * modules + m) * 2 + w
                part = slice(w * K, w * K + K)
                total_ref[l, m, part, :] = kept_ref[l, m, part, :] + decode(codes_ref, index * K, scales, index)


def split_kernel(dim, where_ref, codes_in, kept_in, codes_ref, kept_ref, scales_ref, total_ref):
    add_codes(codes_in, kept_in, total_ref)
    split(dim, total_ref, codes_ref, kept_ref, scales_ref, where_ref)


def products(ins, totals):
    total = None
    for chunk, sums in enumerate(totals):
        add_codes(ins[2 * chunk], ins[2 * chunk + 1], sums)
        part = lax.dot_general(
            sums[0, 0, :K, :], sums[0, 0, K:, :], (((1,), (1,)), ((), ())), precision=HIGH, preferred_element_type=F32
        )
        total = part if total is None else total + part
    return total


def early_kernel(where_ref, tests_in, *refs):
    chunks = (len(refs) - 3) // 3
    sum_ref, tests_ref, sem = refs[2 * chunks], refs[2 * chunks + 1], refs[-1]
    copy = pltpu.make_async_copy(tests_in, tests_ref, sem)
    copy.start()
    sum_ref[...] = products(refs[: 2 * chunks], refs[2 * chunks + 2 : -1])
    copy.wait()


def outer_kernel(where_ref, early_ref, *refs):
    chunks = (len(refs) - 3) // 3
    leave_ref, stay_ref, out_ref = refs[2 * chunks : 2 * chunks + 3]
    out_ref[...] = early_ref[...] + products(refs[: 2 * chunks], refs[2 * chunks + 3 :])
    core = where_ref[0]
    quarter = K // 4
    for y in range(2):
        leave_ref[y] = out_ref[pl.ds(pl.multiple_of((2 * y + 1 - core) * quarter, 8), quarter), :]
        stay_ref[y] = out_ref[pl.ds(pl.multiple_of((2 * y + core) * quarter, 8), quarter), :]


def scores_kernel(flat_ref, tests_ref, out_ref):
    rest = flat_ref[...]
    rows = rest.shape[0]
    parts = []
    for _ in range(3):
        part = rest.astype(BF16)
        parts.append(part)
        rest = rest - part.astype(F32)
    terms = lax.dot_general(
        jnp.concatenate(parts, axis=0), tests_ref[...], (((1,), (1,)), ((), ())), preferred_element_type=F32
    )
    out_ref[...] = terms[2 * rows :] + terms[rows : 2 * rows] + terms[:rows]


def project_kernel(own, first, ahead, after, where_ref, *refs):
    acts, projs, refs = refs[:4], refs[4:8], refs[8:]
    given, refs = refs[:ahead], refs[ahead:]
    proj_bufs, sems, act_bufs = refs[-5:-1], refs[-1], refs[-9:-5]
    outs, fetched = refs[: -9 - after], refs[len(refs) - 9 - after : -9]
    layers, _, total = acts[0].shape
    quarter = total // 4
    width = act_bufs[0].shape[-1]
    pieces = [(s, l, i) for s in range(2) for l in range(layers) for i in range(4)]

    def fetch(index, core, target, sem):
        s, l, i = pieces[index]
        lanes = pl.ds(pl.multiple_of(s * (total // 2) + core * quarter + first, 128), width)
        copy = pltpu.make_async_copy(acts[i].at[l, :, lanes], target, sem)
        copy.start()
        return copy

    core = where_ref[0] if own else 1 - where_ref[0]
    copies = {}
    loads = [pltpu.make_async_copy(projs[i], proj_bufs[i], sems.at[len(pieces) + i]) for i in range(4)]
    for copy in loads:
        copy.start()
    for index in range(ahead, len(pieces)):
        s, l, i = pieces[index]
        copies[index] = fetch(index, core, act_bufs[i].at[s, l], sems.at[index])
    later = [fetch(j, where_ref[0], fetched[j], sems.at[len(pieces) + 4 + j]) for j in range(after)]
    for copy in loads:
        copy.wait()
    for index, (s, l, i) in enumerate(pieces):
        if index in copies:
            copies[index].wait()
        act = act_bufs[i][s, l] if index in copies else given[index][...]
        value = jnp.dot(proj_bufs[i][l], act, preferred_element_type=F32)
        at = 0
        for out_ref in outs:
            span = out_ref.shape[-1] // 2
            out_ref[l, i // 2, i % 2 * K : i % 2 * K + K, s * span : (s + 1) * span] = value[:, at : at + span]
            at += span
    for copy in later:
        copy.wait()


def join_kernel(dim, at, where_ref, own_ref, got_ref, codes_ref, kept_ref, scales_ref, total_ref):
    span, width = own_ref.shape[-1] // 2, total_ref.shape[-1] // 2
    for s in range(2):
        lanes = slice(s * span + at, s * span + at + width)
        total_ref[:, :, :, s * width : (s + 1) * width] = own_ref[:, :, :, lanes] + got_ref[:, :, :, lanes]
    split(dim, total_ref, codes_ref, kept_ref, scales_ref, where_ref)


CHUNKS = ((384, 'sml'), (384, 'msl'), (256, 'sml'))
GROUPS = ((0,), (1, 2))
PLAN = (('send', 0, (0, 1, 2)), ('own', 0, (0, 1, 2)), ('k', 0, 0), ('x', 0, 0), ('k', 1, 0), ('x', 1, 0), ('k', 2, 0), ('x', 2, 0), ('k', 0, 1), ('x', 0, 1), ('k', 1, 1), ('x', 1, 1), ('k', 2, 1), ('x', 2, 1), ('k', 0, 2), ('x', 0, 2), ('k', 2, 2), ('x', 2, 2), ('k', 1, 2), ('x', 1, 2))
AFTER = 4
EARLY = 1
FINISH = tuple(i for kind, i, stage in PLAN if kind == "x" and stage == 2)
BITS = {"s": 2, "m": 4, "l": 8}


def cube_body(
    attn_in, attn_grad, ffn_in, ffn_grad, proj_attn_in, proj_attn_out, proj_ffn_in, proj_ffn_out, test_grads
):
    acts = (attn_grad, attn_in, ffn_grad, ffn_in)
    projs = tuple(w.transpose(0, 2, 1) for w in (proj_attn_out, proj_attn_in, proj_ffn_out, proj_ffn_in))
    acts = tuple(pltpu.with_memory_space_constraint(a, pltpu.HBM) for a in acts)
    projs = tuple(pltpu.with_memory_space_constraint(a, pltpu.HBM) for a in projs)
    me = lax.axis_index("tp")
    core, y, z = me % 2, (me // 2) % 2, me // 4
    where = jnp.stack([core, y, z % 2, z // 2]).astype(jnp.int32)
    smem = pl.BlockSpec(memory_space=pltpu.SMEM)
    vmem = pl.BlockSpec(memory_space=pltpu.VMEM)
    hbm = pl.BlockSpec(memory_space=pltpu.HBM)

    def swap(value, bit):
        return lax.ppermute(value, "tp", [(i, i ^ bit) for i in range(16)])

    def sds(shape, dtype=F32):
        return jax.ShapeDtypeStruct(shape, dtype)

    def call(kernel, ins, in_specs, outs, scratch, cost, limit):
        return pl.pallas_call(
            kernel, out_shape=outs, in_specs=[smem] + in_specs, out_specs=[vmem] * len(outs), scratch_shapes=scratch,
            cost_estimate=pl.CostEstimate(flops=0, bytes_accessed=cost, transcendentals=0),
            compiler_params=pltpu.CompilerParams(vmem_limit_bytes=limit << 20),
        )(where, *ins)

    def outputs(dim, shape):
        layers, modules, _, tokens = shape
        kept = {
            "s": (layers, modules, 2 * K, tokens // 2), "m": (layers, 1, 2 * K, tokens), "l": (1, modules, 2 * K, tokens)
        }[dim]
        groups = kept[0] * kept[1] * 2
        scales = max(8, groups)
        return (sds((groups * K + scales, kept[3]), BF16), sds(kept)), pltpu.VMEM((scales, kept[3]), F32)

    def project(own, chunks, given=(), after=0):
        widths = [sum(CHUNKS[i][0] for i in group) for group in GROUPS]
        first = sum(width for width, _ in CHUNKS[: chunks[0]])
        width = sum(widths)
        layers = acts[0].shape[0]
        scratch = [pltpu.VMEM((2, layers, a.shape[1], width), BF16) for a in acts]
        scratch += [pltpu.VMEM(w.shape, BF16) for w in projs] + [pltpu.SemaphoreType.DMA((8 * layers + 4 + after,))]
        outs = tuple(sds((2, 2, 2 * K, 2 * width)) for width in widths)
        outs += tuple(sds((acts[i % 4].shape[1], width), BF16) for i in range(after))
        results = call(
            functools.partial(project_kernel, own, first, len(given), after), (*acts, *projs, *given),
            [hbm] * 8 + [vmem] * len(given), outs, scratch, 16 << 20, 26,
        )
        return results[: len(widths)], results[len(widths) :]

    def join(index, own, got, dim):
        group = next(g for g in GROUPS if index in g)
        at = sum(CHUNKS[j][0] for j in group if j < index)
        shape = (*own.shape[:3], 2 * CHUNKS[index][0])
        outs, scales = outputs(dim, shape)
        return call(
            functools.partial(join_kernel, dim, at), (own, got), [vmem] * 2, outs, [scales, pltpu.VMEM(shape, F32)],
            4 << 20, 12,
        )

    def exchange(codes, kept, dim):
        outs, scales = outputs(dim, kept.shape)
        return call(
            functools.partial(split_kernel, dim), (codes, kept), [vmem] * 2, outs,
            [scales, pltpu.VMEM(kept.shape, F32)], 4 << 20, 12,
        )

    got, own, state, ready = {}, {}, {}, ()
    for step in PLAN:
        kind, i, stage = step
        if kind == "send":
            sent, ready = project(False, stage, (), AFTER)
            for group, value in zip(GROUPS, sent):
                value = swap(value, 1)
                got.update({j: value for j in group})
        elif kind == "own":
            made, _ = project(True, stage, ready)
            own.update({j: value for group, value in zip(GROUPS, made) for j in group})
            ready = ()
        elif kind == "k" and stage == 0:
            state[i] = join(i, own[i], got[i], CHUNKS[i][1][0])
        elif kind == "k":
            state[i] = exchange(*state[i], CHUNKS[i][1][stage])
        else:
            dim = CHUNKS[i][1][stage]
            state[i] = (swap(state[i][0], BITS[dim]), state[i][1])
    state = [tuple(state[i]) for i in range(len(CHUNKS))]


    before, last = [state[i] for i in FINISH[:EARLY]], [state[i] for i in FINISH[EARLY:]]
    tests = pltpu.with_memory_space_constraint(test_grads, pltpu.HBM)
    early, tests = call(
        early_kernel, (tests, *sum(before, ())), [hbm] + [vmem] * (2 * len(before)),
        (sds((K, K)), sds(tests.shape, tests.dtype)),
        [pltpu.VMEM(k.shape, F32) for _, k in before] + [pltpu.SemaphoreType.DMA], 4 << 20, 12,
    )
    leave, stay = call(
        outer_kernel, (early, *sum(last, ())), [vmem] * (1 + 2 * len(last)), (sds((2, K // 4, K)), sds((2, K // 4, K))),
        [pltpu.VMEM((K, K), F32)] + [pltpu.VMEM(k.shape, F32) for _, k in last], 2 << 20, 12,
    )
    mine = stay + swap(leave, 1)
    here = lax.dynamic_index_in_dim(mine, y, 0, keepdims=False)
    there = swap(lax.dynamic_index_in_dim(mine, 1 - y, 0, keepdims=False), 2)
    first = jnp.where(y == 0, here, there)
    second = jnp.where(y == 0, there, here)
    flat = jnp.stack([first, second]).reshape(2, K // 4 * K)
    scores = pl.pallas_call(
        scores_kernel, out_shape=sds((2, test_grads.shape[0])), in_specs=[vmem] * 2, out_specs=vmem, name="scores",
        compiler_params=pltpu.CompilerParams(vmem_limit_bytes=12 << 20),
    )(flat, tests)
    for bit in (1, 2, 4, 8):
        scores = scores + swap(scores, bit)
    return scores


def cube(*args):
    return cube_body(*args)


def shards(
    attn_in, attn_grad, ffn_in, ffn_grad, proj_attn_in, proj_attn_out, proj_ffn_in, proj_ffn_out, test_grads
):
    layers, _, total = attn_in.shape
    devices = lax.axis_size("tp")
    modules = ((attn_grad, proj_attn_out, attn_in, proj_attn_in), (ffn_grad, proj_ffn_out, ffn_in, proj_ffn_in))
    columns = []
    for layer in range(layers):
        for grad, out, source, into in modules:
            for act, weight in ((grad, out), (source, into)):
                columns.append(
                    lax.dot_general(
                        weight[layer], act[layer], (((0,), (0,)), ((), ())), preferred_element_type=F32
                    )
                )
    rows = total // devices
    projected = lax.psum_scatter(jnp.concatenate(columns), "tp", scatter_dimension=1, tiled=True)
    token = lax.axis_index("tp") * rows + jnp.arange(rows, dtype=jnp.int32)
    member = (token // LEN)[None, :] == jnp.arange(SEQS, dtype=jnp.int32)[:, None]
    pairs = projected.reshape(2 * layers, 2, K, rows)
    grads = jnp.where(member[:, None, None, :], pairs[None, :, 0], 0.0)
    outer = jnp.einsum("snat,nbt->snab", grads, pairs[:, 1], precision=HIGH)
    flat = outer.reshape(SEQS, devices, -1).transpose(1, 0, 2)
    flat = flat.reshape(devices, -1)
    owned = lax.psum_scatter(flat, "tp", scatter_dimension=0, tiled=True).reshape(SEQS, -1)
    scores = lax.dot_general(
        owned, test_grads.astype(F32), (((1,), (1,)), ((), ())), precision=HIGH, preferred_element_type=F32
    )
    return lax.psum(scores, "tp")


def solution(mesh):
    placed = (P(None, "tp", "grp"),) * 4 + (P(None, "tp", None),) * 4 + (P(None, "tp"),)
    cubic = mesh.shape["tp"] == 16
    return jax.shard_map(
        cube if cubic else shards, mesh=mesh, in_specs=placed, out_specs=P("grp", None), check_vma=False
    )
```

```python
import functools

import jax
import jax.numpy as jnp
from jax import lax
from jax.experimental import pallas as pl
from jax.experimental.pallas import tpu as pltpu
from jax.sharding import PartitionSpec as P


LEN = 2048
SEQS = 2
K = 64
F32 = jnp.float32
BF16 = jnp.bfloat16
SPAN = 250.0
HIGH = lax.Precision.HIGHEST


def encode(values, codes_ref, row, scales_ref, index):
    top = jnp.max(jnp.abs(values), axis=0, keepdims=True)
    scale = (top * 1.015625).astype(BF16).astype(F32)
    scales_ref[index : index + 1, :] = scale
    factor = jnp.where(scale > 2e-36, SPAN / jnp.maximum(scale, 2e-36), 0.0)
    power = jnp.exp2(jnp.abs(values) * factor - 0.5 * SPAN)
    codes_ref[row : row + K, :] = jnp.where(values < 0, -power, power).astype(BF16)


def decode(codes_ref, row, scales, index):
    codes = codes_ref[row : row + K, :].astype(F32)
    scale = scales[index : index + 1, :] * (1.0 / SPAN)
    size = (jnp.log2(jnp.abs(codes)) + 0.5 * SPAN) * scale
    return jnp.where(codes < 0, -size, size)


def encode_groups(groups, codes_ref, scales_ref):
    scales_ref[...] = jnp.zeros_like(scales_ref)
    for index, values in enumerate(groups):
        encode(values, codes_ref, index * K, scales_ref, index)
    codes_ref[len(groups) * K :, :] = scales_ref[...].astype(BF16)


def split(dim, total_ref, codes_ref, kept_ref, scales_ref, where_ref):
    layers, modules, _, tokens = total_ref.shape
    mine = where_ref[" sml".index(dim)]
    other = 1 - mine
    if dim == "s":
        width = tokens // 2
        leave = pl.ds(pl.multiple_of(other * width, 128), width)
        stay = pl.ds(pl.multiple_of(mine * width, 128), width)
        groups = [(l, m, w, leave) for l in range(layers) for m in range(modules) for w in range(2)]
    elif dim == "m":
        groups = [(l, other, w, slice(None)) for l in range(layers) for w in range(2)]
    else:
        groups = [(other, m, w, slice(None)) for m in range(modules) for w in range(2)]
    encode_groups(
        [total_ref[l, m, w * K : w * K + K, lanes] for l, m, w, lanes in groups], codes_ref, scales_ref
    )
    if dim == "s":
        kept_ref[...] = total_ref[:, :, :, stay]
    elif dim == "m":
        for l in range(layers):
            kept_ref[l, 0] = total_ref[l, mine]
    else:
        kept_ref[0] = total_ref[mine]


def add_codes(codes_ref, kept_ref, total_ref):
    layers, modules, _, _ = kept_ref.shape
    rows = layers * modules * 2 * K
    scales = codes_ref[rows:, :].astype(F32)
    for l in range(layers):
        for m in range(modules):
            for w in range(2):
                index = (l * modules + m) * 2 + w
                part = slice(w * K, w * K + K)
                total_ref[l, m, part, :] = kept_ref[l, m, part, :] + decode(codes_ref, index * K, scales, index)


def split_kernel(dim, where_ref, codes_in, kept_in, codes_ref, kept_ref, scales_ref, total_ref):
    add_codes(codes_in, kept_in, total_ref)
    split(dim, total_ref, codes_ref, kept_ref, scales_ref, where_ref)


def products(ins, totals):
    total = None
    for chunk, sums in enumerate(totals):
        add_codes(ins[2 * chunk], ins[2 * chunk + 1], sums)
        part = lax.dot_general(
            sums[0, 0, :K, :], sums[0, 0, K:, :], (((1,), (1,)), ((), ())), precision=HIGH, preferred_element_type=F32
        )
        total = part if total is None else total + part
    return total


def early_kernel(where_ref, tests_in, *refs):
    chunks = (len(refs) - 3) // 3
    sum_ref, tests_ref, sem = refs[2 * chunks], refs[2 * chunks + 1], refs[-1]
    copy = pltpu.make_async_copy(tests_in, tests_ref, sem)
    copy.start()
    sum_ref[...] = products(refs[: 2 * chunks], refs[2 * chunks + 2 : -1])
    copy.wait()


def outer_kernel(where_ref, early_ref, *refs):
    chunks = (len(refs) - 3) // 3
    leave_ref, stay_ref, out_ref = refs[2 * chunks : 2 * chunks + 3]
    out_ref[...] = early_ref[...] + products(refs[: 2 * chunks], refs[2 * chunks + 3 :])
    core = where_ref[0]
    quarter = K // 4
    for y in range(2):
        leave_ref[y] = out_ref[pl.ds(pl.multiple_of((2 * y + 1 - core) * quarter, 8), quarter), :]
        stay_ref[y] = out_ref[pl.ds(pl.multiple_of((2 * y + core) * quarter, 8), quarter), :]


def scores_kernel(flat_ref, tests_ref, out_ref):
    rest = flat_ref[...]
    rows = rest.shape[0]
    parts = []
    for _ in range(3):
        part = rest.astype(BF16)
        parts.append(part)
        rest = rest - part.astype(F32)
    terms = lax.dot_general(
        jnp.concatenate(parts, axis=0), tests_ref[...], (((1,), (1,)), ((), ())), preferred_element_type=F32
    )
    out_ref[...] = terms[2 * rows :] + terms[rows : 2 * rows] + terms[:rows]


def project_kernel(own, first, ahead, after, where_ref, *refs):
    acts, projs, refs = refs[:4], refs[4:8], refs[8:]
    given, refs = refs[:ahead], refs[ahead:]
    proj_bufs, sems, act_bufs = refs[-5:-1], refs[-1], refs[-9:-5]
    outs, fetched = refs[: -9 - after], refs[len(refs) - 9 - after : -9]
    layers, _, total = acts[0].shape
    quarter = total // 4
    width = act_bufs[0].shape[-1]
    pieces = [(s, l, i) for s in range(2) for l in range(layers) for i in range(4)]

    def fetch(index, core, target, sem):
        s, l, i = pieces[index]
        lanes = pl.ds(pl.multiple_of(s * (total // 2) + core * quarter + first, 128), width)
        copy = pltpu.make_async_copy(acts[i].at[l, :, lanes], target, sem)
        copy.start()
        return copy

    core = where_ref[0] if own else 1 - where_ref[0]
    copies = {}
    loads = [pltpu.make_async_copy(projs[i], proj_bufs[i], sems.at[len(pieces) + i]) for i in range(4)]
    for copy in loads:
        copy.start()
    for index in range(ahead, len(pieces)):
        s, l, i = pieces[index]
        copies[index] = fetch(index, core, act_bufs[i].at[s, l], sems.at[index])
    later = [fetch(j, where_ref[0], fetched[j], sems.at[len(pieces) + 4 + j]) for j in range(after)]
    for copy in loads:
        copy.wait()
    for index, (s, l, i) in enumerate(pieces):
        if index in copies:
            copies[index].wait()
        act = act_bufs[i][s, l] if index in copies else given[index][...]
        value = jnp.dot(proj_bufs[i][l], act, preferred_element_type=F32)
        at = 0
        for out_ref in outs:
            span = out_ref.shape[-1] // 2
            out_ref[l, i // 2, i % 2 * K : i % 2 * K + K, s * span : (s + 1) * span] = value[:, at : at + span]
            at += span
    for copy in later:
        copy.wait()


def join_kernel(dim, at, width, where_ref, own_ref, got_ref, codes_ref, kept_ref, scales_ref):
    span = own_ref.shape[-1] // 2
    layers, modules = own_ref.shape[:2]
    scales_ref[...] = jnp.zeros_like(scales_ref)

    def total(l, m, w, lanes):
        rows = slice(w * K, w * K + K)
        return own_ref[l, m, rows, lanes] + got_ref[l, m, rows, lanes]

    if dim == "s":
        mine = where_ref[1]
        leave = pl.ds(pl.multiple_of((1 - mine) * span + at, 128), width)
        stay = pl.ds(pl.multiple_of(mine * span + at, 128), width)
        groups = [(l, m, w) for l in range(layers) for m in range(modules) for w in range(2)]
        for index, (l, m, w) in enumerate(groups):
            encode(total(l, m, w, leave), codes_ref, index * K, scales_ref, index)
        for l, m, w in groups:
            kept_ref[l, m, w * K : w * K + K, :] = total(l, m, w, stay)
    else:
        mine = where_ref[2]
        for s in range(2):
            lanes, place = slice(s * span + at, s * span + at + width), slice(s * width, (s + 1) * width)
            for l in range(layers):
                for w in range(2):
                    index = l * 2 + w
                    encode(
                        total(l, 1 - mine, w, lanes), codes_ref.at[:, place], index * K, scales_ref.at[:, place], index
                    )
                    kept_ref[l, 0, w * K : w * K + K, place] = total(l, mine, w, lanes)
    codes_ref[codes_ref.shape[0] - scales_ref.shape[0] :, :] = scales_ref[...].astype(BF16)


CHUNKS = ((384, 'sml'), (384, 'msl'), (256, 'sml'))
GROUPS = ((0,), (1, 2))
PLAN = (('send', 0, (0, 1, 2)), ('own', 0, (0, 1, 2)), ('k', 0, 0), ('x', 0, 0), ('k', 1, 0), ('x', 1, 0), ('k', 2, 0), ('x', 2, 0), ('k', 0, 1), ('x', 0, 1), ('k', 1, 1), ('x', 1, 1), ('k', 2, 1), ('x', 2, 1), ('k', 0, 2), ('x', 0, 2), ('k', 2, 2), ('x', 2, 2), ('k', 1, 2), ('x', 1, 2))
AFTER = 5
EARLY = 1
FINISH = tuple(i for kind, i, stage in PLAN if kind == "x" and stage == 2)
BITS = {"s": 2, "m": 4, "l": 8}


def cube_body(
    attn_in, attn_grad, ffn_in, ffn_grad, proj_attn_in, proj_attn_out, proj_ffn_in, proj_ffn_out, test_grads
):
    acts = (attn_grad, attn_in, ffn_grad, ffn_in)
    projs = tuple(w.transpose(0, 2, 1) for w in (proj_attn_out, proj_attn_in, proj_ffn_out, proj_ffn_in))
    acts = tuple(pltpu.with_memory_space_constraint(a, pltpu.HBM) for a in acts)
    projs = tuple(pltpu.with_memory_space_constraint(a, pltpu.HBM) for a in projs)
    me = lax.axis_index("tp")
    core, y, z = me % 2, (me // 2) % 2, me // 4
    where = jnp.stack([core, y, z % 2, z // 2]).astype(jnp.int32)
    smem = pl.BlockSpec(memory_space=pltpu.SMEM)
    vmem = pl.BlockSpec(memory_space=pltpu.VMEM)
    hbm = pl.BlockSpec(memory_space=pltpu.HBM)

    def swap(value, bit):
        return lax.ppermute(value, "tp", [(i, i ^ bit) for i in range(16)])

    def sds(shape, dtype=F32):
        return jax.ShapeDtypeStruct(shape, dtype)

    def call(kernel, ins, in_specs, outs, scratch, cost, limit):
        return pl.pallas_call(
            kernel, out_shape=outs, in_specs=[smem] + in_specs, out_specs=[vmem] * len(outs), scratch_shapes=scratch,
            cost_estimate=pl.CostEstimate(flops=0, bytes_accessed=cost, transcendentals=0),
            compiler_params=pltpu.CompilerParams(vmem_limit_bytes=limit << 20),
        )(where, *ins)

    def outputs(dim, shape):
        layers, modules, _, tokens = shape
        kept = {
            "s": (layers, modules, 2 * K, tokens // 2), "m": (layers, 1, 2 * K, tokens), "l": (1, modules, 2 * K, tokens)
        }[dim]
        groups = kept[0] * kept[1] * 2
        scales = max(8, groups)
        return (sds((groups * K + scales, kept[3]), BF16), sds(kept)), pltpu.VMEM((scales, kept[3]), F32)

    def project(own, chunks, given=(), after=0):
        widths = [sum(CHUNKS[i][0] for i in group) for group in GROUPS]
        first = sum(width for width, _ in CHUNKS[: chunks[0]])
        width = sum(widths)
        layers = acts[0].shape[0]
        scratch = [pltpu.VMEM((2, layers, a.shape[1], width), BF16) for a in acts]
        scratch += [pltpu.VMEM(w.shape, BF16) for w in projs] + [pltpu.SemaphoreType.DMA((8 * layers + 4 + after,))]
        outs = tuple(sds((2, 2, 2 * K, 2 * width)) for width in widths)
        outs += tuple(sds((acts[i % 4].shape[1], width), BF16) for i in range(after))
        results = call(
            functools.partial(project_kernel, own, first, len(given), after), (*acts, *projs, *given),
            [hbm] * 8 + [vmem] * len(given), outs, scratch, 16 << 20, 26,
        )
        return results[: len(widths)], results[len(widths) :]

    def join(index, own, got, dim):
        group = next(g for g in GROUPS if index in g)
        at = sum(CHUNKS[j][0] for j in group if j < index)
        shape = (*own.shape[:3], 2 * CHUNKS[index][0])
        outs, scales = outputs(dim, shape)
        return call(
            functools.partial(join_kernel, dim, at, CHUNKS[index][0]), (own, got), [vmem] * 2, outs, [scales],
            4 << 20, 12,
        )

    def exchange(codes, kept, dim):
        outs, scales = outputs(dim, kept.shape)
        return call(
            functools.partial(split_kernel, dim), (codes, kept), [vmem] * 2, outs,
            [scales, pltpu.VMEM(kept.shape, F32)], 4 << 20, 12,
        )

    got, own, state, ready = {}, {}, {}, ()
    for step in PLAN:
        kind, i, stage = step
        if kind == "send":
            sent, ready = project(False, stage, (), AFTER)
            for group, value in zip(GROUPS, sent):
                value = swap(value, 1)
                got.update({j: value for j in group})
        elif kind == "own":
            made, _ = project(True, stage, ready)
            own.update({j: value for group, value in zip(GROUPS, made) for j in group})
            ready = ()
        elif kind == "k" and stage == 0:
            state[i] = join(i, own[i], got[i], CHUNKS[i][1][0])
        elif kind == "k":
            state[i] = exchange(*state[i], CHUNKS[i][1][stage])
        else:
            dim = CHUNKS[i][1][stage]
            state[i] = (swap(state[i][0], BITS[dim]), state[i][1])
    state = [tuple(state[i]) for i in range(len(CHUNKS))]


    before, last = [state[i] for i in FINISH[:EARLY]], [state[i] for i in FINISH[EARLY:]]
    tests = pltpu.with_memory_space_constraint(test_grads, pltpu.HBM)
    early, tests = call(
        early_kernel, (tests, *sum(before, ())), [hbm] + [vmem] * (2 * len(before)),
        (sds((K, K)), sds(tests.shape, tests.dtype)),
        [pltpu.VMEM(k.shape, F32) for _, k in before] + [pltpu.SemaphoreType.DMA], 4 << 20, 12,
    )
    leave, stay = call(
        outer_kernel, (early, *sum(last, ())), [vmem] * (1 + 2 * len(last)), (sds((2, K // 4, K)), sds((2, K // 4, K))),
        [pltpu.VMEM((K, K), F32)] + [pltpu.VMEM(k.shape, F32) for _, k in last], 2 << 20, 12,
    )
    mine = stay + swap(leave, 1)
    here = lax.dynamic_index_in_dim(mine, y, 0, keepdims=False)
    there = swap(lax.dynamic_index_in_dim(mine, 1 - y, 0, keepdims=False), 2)
    first = jnp.where(y == 0, here, there)
    second = jnp.where(y == 0, there, here)
    flat = jnp.stack([first, second]).reshape(2, K // 4 * K)
    scores = pl.pallas_call(
        scores_kernel, out_shape=sds((2, test_grads.shape[0])), in_specs=[vmem] * 2, out_specs=vmem, name="scores",
        compiler_params=pltpu.CompilerParams(vmem_limit_bytes=12 << 20),
    )(flat, tests)
    for bit in (1, 2, 4, 8):
        scores = scores + swap(scores, bit)
    return scores


def cube(*args):
    return cube_body(*args)


def shards(
    attn_in, attn_grad, ffn_in, ffn_grad, proj_attn_in, proj_attn_out, proj_ffn_in, proj_ffn_out, test_grads
):
    layers, _, total = attn_in.shape
    devices = lax.axis_size("tp")
    modules = ((attn_grad, proj_attn_out, attn_in, proj_attn_in), (ffn_grad, proj_ffn_out, ffn_in, proj_ffn_in))
    columns = []
    for layer in range(layers):
        for grad, out, source, into in modules:
            for act, weight in ((grad, out), (source, into)):
                columns.append(
                    lax.dot_general(
                        weight[layer], act[layer], (((0,), (0,)), ((), ())), preferred_element_type=F32
                    )
                )
    rows = total // devices
    projected = lax.psum_scatter(jnp.concatenate(columns), "tp", scatter_dimension=1, tiled=True)
    token = lax.axis_index("tp") * rows + jnp.arange(rows, dtype=jnp.int32)
    member = (token // LEN)[None, :] == jnp.arange(SEQS, dtype=jnp.int32)[:, None]
    pairs = projected.reshape(2 * layers, 2, K, rows)
    grads = jnp.where(member[:, None, None, :], pairs[None, :, 0], 0.0)
    outer = jnp.einsum("snat,nbt->snab", grads, pairs[:, 1], precision=HIGH)
    flat = outer.reshape(SEQS, devices, -1).transpose(1, 0, 2)
    flat = flat.reshape(devices, -1)
    owned = lax.psum_scatter(flat, "tp", scatter_dimension=0, tiled=True).reshape(SEQS, -1)
    scores = lax.dot_general(
        owned, test_grads.astype(F32), (((1,), (1,)), ((), ())), precision=HIGH, preferred_element_type=F32
    )
    return lax.psum(scores, "tp")


def solution(mesh):
    placed = (P(None, "tp", "grp"),) * 4 + (P(None, "tp", None),) * 4 + (P(None, "tp"),)
    cubic = mesh.shape["tp"] == 16
    return jax.shard_map(
        cube if cubic else shards, mesh=mesh, in_specs=placed, out_specs=P("grp", None), check_vma=False
    )
```
